32 devices in a mesh: blk: 2 (over y), uly: 16 (over z, x, core).
Axes of the slice: x: 2, y: 2, z: 4, core: 2. Of those that a mesh axis runs over, the one named last changes fastest.
Arguments:
- queries: bfloat16 [4096, 2048], P(('blk', 'uly')), may hold values from -8 to 8
- keys: bfloat16 [4096, 2048], P(('blk', 'uly')), may hold values from -8 to 8
- values: bfloat16 [4096, 2048], P(('blk', 'uly')), may hold values from -6 to 6
- grad_out: bfloat16 [4096, 2048], P(('blk', 'uly')), may hold values from -6 to 6
- doc_start: int32 [32], replicated, may hold values from 0 to 3968, as said below
Outputs:
- grad_queries: bfloat16 [4096, 2048], P(('blk', 'uly'))
- grad_keys: bfloat16 [4096, 2048], P(('blk', 'uly'))
- grad_values: bfloat16 [4096, 2048], P(('blk', 'uly'))
The draws below stay inside these ranges and needn't reach their ends.
Inputs may be any that keep to these rules, and one draw needn't show every extreme that they name: `doc_start`: each entry is the first position of its block's document, so documents are runs of whole blocks; no document is longer than 8 blocks and one is exactly 8; a document crosses every boundary between groups of 2048 positions and starts at most 7 blocks before it, at one boundary exactly 7; the last block starts a document.
All inputs are finite; a program needn't handle non-finite values.
Results may differ from the reference program's by a relative error of at most 0.0051.
Values may be sent and summed in bfloat16 or wider, within the bound.
A program may use at most 64 MiB of HBM per device.

```python
import math
from functools import partial
import jax
import jax.numpy as jnp
from jax import lax

HD = 128
ROWS = 128
BLOCK = 128
MAXB = 8
HEADS = 16
SEQ = 4096
NBLOCKS = 32
N_BLK = 2
N_ULY = 16


def base_draw(key):
    return jnp.clip(jax.random.normal(key, (SEQ, HEADS * HD), jnp.float32), -4.0, 4.0)


def draw_queries(key, part):
    base = base_draw(jax.random.fold_in(key, 1))
    return base.astype(jnp.bfloat16)


def draw_keys(key, part):
    base = base_draw(jax.random.fold_in(key, 2))
    return base.astype(jnp.bfloat16)


def draw_doc_start(key, part):
    group_blocks = N_ULY * ROWS // BLOCK
    bounds = N_BLK - 1
    key_reach, key_before, key_extra, key_flags = jax.random.split(key, 4)
    reach = jax.random.randint(key_reach, (), 0, bounds)
    which = jnp.arange(bounds)
    before = jax.random.randint(key_before, (bounds,), 1, MAXB)
    before = jnp.where(which == reach, MAXB - 1, before)
    extra = jax.random.randint(key_extra, (bounds,), 0, MAXB)
    length = before + 1 + extra % (MAXB - before)
    length = jnp.where(which == reach, MAXB, length)
    starts_at = (which + 1) * group_blocks - before
    ends_at = starts_at + length
    index = jnp.arange(NBLOCKS)
    inside = jnp.any((index[:, None] > starts_at[None, :]) & (index[:, None] < ends_at[None, :]), axis=1)
    edge = jnp.any((index[:, None] == starts_at[None, :]) | (index[:, None] == ends_at[None, :]), axis=1)
    flags = jax.random.randint(key_flags, (NBLOCKS,), 0, 3) == 0
    flags = jnp.where(inside, False, jnp.where(edge, True, flags))
    flags = flags.at[0].set(True).at[NBLOCKS - 1].set(True)

    def walk(carry, item):
        current, run = carry
        flag, position = item
        begin = flag | (run >= MAXB)
        current = jnp.where(begin, position, current)
        run = jnp.where(begin, 1, run + 1)
        return ((current, run), current)
    _, starts = lax.scan(walk, (jnp.int32(0), jnp.int32(0)), (flags, index.astype(jnp.int32)))
    return (starts * BLOCK).astype(jnp.int32)


def shard_levels(key, dims, cuts, smallest, high):
    loudness, own = 1.0, jax.random.fold_in(key, 6)
    for dim, shards_of in cuts:
        heights = jnp.exp(jax.random.uniform(jax.random.fold_in(own, dim), (shards_of,), jnp.float32, smallest / len(cuts), high / len(cuts)))
        loudness = loudness * jnp.repeat(heights, dims[dim] // shards_of).reshape([-1 if axis == dim else 1 for axis in range(len(dims))])
    return loudness


def bell_draw(stream_key, shape, spread, most, shards=(), held_as=jnp.bfloat16):
    entries = spread * jax.random.normal(stream_key, shape, jnp.float32)
    if shards:
        entries = entries * shard_levels(stream_key, shape, shards, -0.22, 0.18)
    return jnp.clip(entries, -most, most).astype(held_as)


def setup_inputs(seed: int = 0) -> dict:
    key_list = jax.random.split(jax.random.key(seed), 6)
    return {
        "queries": draw_queries(jax.random.fold_in(key_list[5], 71), 0),
        "keys": draw_keys(jax.random.fold_in(key_list[5], 71), 0),
        "values": bell_draw(key_list[2], (SEQ, HEADS * HD), 1.0, 6.0, ((0, 32),)),
        "grad_out": bell_draw(key_list[3], (SEQ, HEADS * HD), 1.0, 6.0, ((0, 32),)),
        "doc_start": draw_doc_start(jax.random.fold_in(key_list[5], 71), 0),
    }


def head_grads(docs, arrays):
    q_head, k_head, v_head, d_head = arrays
    tile = 4 * BLOCK
    window = tile + MAXB * BLOCK
    scale = 1.0 / math.sqrt(HD)

    def step(carry, t):
        grad_k, grad_v = carry
        q_start = (t * tile).astype(jnp.int32)
        w_start = jnp.clip(q_start - MAXB * BLOCK, 0, SEQ - window).astype(jnp.int32)
        q_rows = lax.dynamic_slice_in_dim(q_head, q_start, tile, 0)
        d_rows = lax.dynamic_slice_in_dim(d_head, q_start, tile, 0)
        k_rows = lax.dynamic_slice_in_dim(k_head, w_start, window, 0)
        v_rows = lax.dynamic_slice_in_dim(v_head, w_start, window, 0)
        q_doc = lax.dynamic_slice_in_dim(docs, q_start, tile, 0)
        k_doc = lax.dynamic_slice_in_dim(docs, w_start, window, 0)
        q_pos = q_start + jnp.arange(tile, dtype=jnp.int32)
        k_pos = w_start + jnp.arange(window, dtype=jnp.int32)
        allowed = (q_doc[:, None] == k_doc[None, :]) & (k_pos[None, :] <= q_pos[:, None])
        score = jnp.dot(q_rows, k_rows.T, preferred_element_type=jnp.float32) * scale
        score = jnp.where(allowed, score, -jnp.inf)
        top = lax.optimization_barrier(jnp.max(score, axis=1, keepdims=True))
        lse = top + jnp.log(lax.optimization_barrier(jnp.sum(jnp.exp(score - top), axis=1, keepdims=True)))
        prob = jnp.exp(score - lse)
        dprob = jnp.dot(d_rows, v_rows.T, preferred_element_type=jnp.float32)
        delta = lax.optimization_barrier(jnp.sum(prob * dprob, axis=1, keepdims=True))
        dscore = (prob * (dprob - delta) * scale).astype(jnp.bfloat16)
        prob_low = prob.astype(jnp.bfloat16)
        grad_q = jnp.dot(dscore, k_rows, preferred_element_type=jnp.float32).astype(jnp.bfloat16)
        part_k = jnp.dot(dscore.T, q_rows, preferred_element_type=jnp.float32)
        part_v = jnp.dot(prob_low.T, d_rows, preferred_element_type=jnp.float32)
        grad_k = lax.dynamic_update_slice_in_dim(grad_k, lax.dynamic_slice_in_dim(grad_k, w_start, window, 0) + part_k, w_start, 0)
        grad_v = lax.dynamic_update_slice_in_dim(grad_v, lax.dynamic_slice_in_dim(grad_v, w_start, window, 0) + part_v, w_start, 0)
        return ((grad_k, grad_v), grad_q)
    start = (jnp.zeros((SEQ, HD), jnp.float32), jnp.zeros((SEQ, HD), jnp.float32))
    (grad_k, grad_v), grad_q = lax.scan(step, start, jnp.arange(SEQ // tile, dtype=jnp.int32))
    return (grad_q.reshape(SEQ, HD), grad_k.astype(jnp.bfloat16), grad_v.astype(jnp.bfloat16))

def reference(queries, keys, values, grad_out, doc_start):
    heads = queries.shape[1] // HD
    docs = jnp.repeat(doc_start, BLOCK)

    def split_heads(array):
        return array.reshape(SEQ, heads, HD).transpose(1, 0, 2)

    def merge_heads(array):
        return array.transpose(1, 0, 2).reshape(SEQ, heads * HD)
    grad_q, grad_k, grad_v = lax.map(partial(head_grads, docs), (split_heads(queries), split_heads(keys), split_heads(values), split_heads(grad_out)))
    return (merge_heads(grad_q), merge_heads(grad_k), merge_heads(grad_v))
```

```python
import functools
import math

import jax
import jax.numpy as jnp
from jax import lax
from jax.experimental import pallas as pl
from jax.experimental.pallas import tpu as pltpu
from jax.sharding import PartitionSpec as P

MAXB = 8
MESH = pl.DeviceIdType.MESH


def nt_dot(a, b):
    return lax.dot_general(a, b, (((1,), (1,)), ((), ())), preferred_element_type=jnp.float32)


def tn_dot(a, b):
    return lax.dot_general(a, b, (((0,), (0,)), ((), ())), preferred_element_type=jnp.float32)


def nn_dot(a, b):
    return lax.dot_general(a, b, (((1,), (0,)), ((), ())), preferred_element_type=jnp.float32)


def kernel(
    n, groups, rows, width,
    docs, q_in, k_in, v_in, d_in,
    gq, gk, gv,
    ext_k, ext_v, q_all, d_all, dk_acc, dv_acc, dq_low, dk_low, dv_low,
    give_k, give_v, back_k, back_v,
    own_sem, in_send, in_recv, far_send, far_recv, back_send, back_recv,
    out_own, out_send, out_recv,
):
    blk = lax.axis_index("blk")
    me = lax.axis_index("uly")
    reach = MAXB - 1
    far = reach * rows
    tail = far + (n - reach) * rows
    scale = 1.0 / math.sqrt(width)

    barrier = pltpu.get_barrier_semaphore()

    def greet(s, carry):
        pl.semaphore_signal(
            barrier, inc=1, device_id=(blk, lax.rem(me + s, n)), device_id_type=MESH
        )
        return carry

    lax.fori_loop(1, n, greet, 0)

    beside = sorted({1, groups - 1} - {0, groups})
    for by in beside:
        pl.semaphore_signal(
            barrier, inc=1, device_id=(lax.rem(blk + by, groups), me), device_id_type=MESH
        )

    def columns(ref, head):
        return ref.at[:, pl.ds(pl.multiple_of(head * width, width), width)]

    def block(ref, base, index):
        return ref.at[pl.ds(pl.multiple_of(base + index * rows, rows), rows), :]

    streams = ((k_in, ext_k, far), (q_in, q_all, 0), (v_in, ext_v, far), (d_in, d_all, 0))

    own = [
        pltpu.make_async_copy(columns(src, me), block(dst, base, me), own_sem.at[a])
        for a, (src, dst, base) in enumerate(streams)
    ]
    for copy in own:
        copy.start()

    pl.semaphore_wait(barrier, n - 1 + len(beside))

    for a, (src, dst, base) in enumerate(streams):
        def send(s, carry, a=a, src=src, dst=dst, base=base):
            to = lax.rem(me + s, n)
            pltpu.make_async_remote_copy(
                src_ref=columns(src, to),
                dst_ref=block(dst, base, me),
                send_sem=in_send.at[a],
                recv_sem=in_recv.at[a],
                device_id=(blk, to),
                device_id_type=MESH,
            ).start()
            return carry

        lax.fori_loop(1, n, send, 0)

    dk_acc[...] = jnp.zeros_like(dk_acc)
    dv_acc[...] = jnp.zeros_like(dv_acc)

    @pl.when(blk == 0)
    def _():
        ext_k[pl.ds(0, far), :] = jnp.zeros((far, width), ext_k.dtype)
        ext_v[pl.ds(0, far), :] = jnp.zeros((far, width), ext_v.dtype)

    def wait_bytes(sem):
        part = q_all.at[pl.ds(0, (n - 1) * rows), :]
        pltpu.make_async_copy(part, part, sem).wait()

    def forward(ref, a):
        return pltpu.make_async_remote_copy(
            src_ref=ref.at[pl.ds(tail, far), :],
            dst_ref=ref.at[pl.ds(0, far), :],
            send_sem=far_send.at[a],
            recv_sem=far_recv.at[a],
            device_id=(blk + 1, me),
            device_id_type=MESH,
        )

    def arrived(a):
        own[a].wait()
        wait_bytes(in_recv.at[a])

    arrived(0)

    @pl.when(blk < groups - 1)
    def _():
        forward(ext_k, 0).start()

    arrived(1)
    arrived(2)

    @pl.when(blk < groups - 1)
    def _():
        forward(ext_v, 1).start()

    arrived(3)

    @pl.when(blk > 0)
    def _():
        forward(ext_k, 0).wait_recv()
        forward(ext_v, 1).wait_recv()

    window = MAXB * rows
    key_at = lax.broadcasted_iota(jnp.int32, (rows, rows), 0)
    query_at = lax.broadcasted_iota(jnp.int32, (rows, rows), 1)

    def attend(i):
        here = pl.ds(pl.multiple_of(i * rows, rows), rows)
        span = pl.ds(pl.multiple_of(i * rows, rows), window)
        q = q_all[here, :]
        d = d_all[here, :]
        k = ext_k[span, :]
        v = ext_v[span, :]
        score = nt_dot(k, q)
        dprob = nt_dot(v, d)
        mine = blk * n + i
        doc = docs[mine]
        parts = []
        for t in range(reach):
            other = mine - reach + t
            same = (docs[jnp.maximum(other, 0)] == doc) & (other >= 0)
            parts.append(score[t * rows : (t + 1) * rows] + jnp.where(same, 0.0, -1e30))
        parts.append(jnp.where(key_at <= query_at, score[reach * rows :], -1e30))
        score = jnp.concatenate(parts, 0)
        top = jnp.max(score, axis=0, keepdims=True)
        weight = jnp.exp((score - top) * scale)
        share = 1.0 / jnp.sum(weight, axis=0, keepdims=True)
        delta = jnp.sum(weight * dprob, axis=0, keepdims=True) * share
        prob = weight * share
        dscore = (prob * ((dprob - delta) * scale)).astype(jnp.bfloat16)
        dv_acc[span, :] += nn_dot(prob.astype(jnp.bfloat16), d)
        dk_acc[span, :] += nn_dot(dscore, q)
        dq_low[here, :] = tn_dot(dscore, k).astype(jnp.bfloat16)

    def give(src, dst, a, i):
        @pl.when(i != me)
        def _():
            pltpu.make_async_remote_copy(
                src_ref=block(src, 0, i),
                dst_ref=columns(dst, me),
                send_sem=out_send.at[a],
                recv_sem=out_recv.at[a],
                device_id=(blk, i),
                device_id_type=MESH,
            ).start()

    def keep(src, dst, a):
        return pltpu.make_async_copy(block(src, 0, me), columns(dst, me), out_own.at[a])

    def run(first, count):
        def order(s):
            return first + lax.rem(me + s, count)

        def step(s, carry):
            @pl.when(s > 0)
            def _():
                give(dq_low, gq, 0, order(s + count - 1))

            attend(order(s))
            return carry

        lax.fori_loop(0, count, step, 0)
        give(dq_low, gq, 0, order(count - 1))

    run(0, reach)

    def handing(src, dst, a):
        return pltpu.make_async_remote_copy(
            src_ref=src,
            dst_ref=dst,
            send_sem=back_send.at[a],
            recv_sem=back_recv.at[a],
            device_id=(blk - 1, me),
            device_id_type=MESH,
        )

    @pl.when(blk > 0)
    def _():
        give_k[...] = dk_acc[pl.ds(0, far), :].astype(jnp.bfloat16)
        give_v[...] = dv_acc[pl.ds(0, far), :].astype(jnp.bfloat16)
        handing(give_k, back_k, 0).start()
        handing(give_v, back_v, 1).start()

    run(reach, n - reach)

    keep(dq_low, gq, 0).start()

    @pl.when(blk < groups - 1)
    def _():
        handing(give_k, back_k, 0).wait_recv()
        handing(give_v, back_v, 1).wait_recv()
        dk_acc[pl.ds(tail, far), :] += back_k[...].astype(jnp.float32)
        dv_acc[pl.ds(tail, far), :] += back_v[...].astype(jnp.float32)

    dk_low[...] = dk_acc[pl.ds(far, n * rows), :].astype(jnp.bfloat16)
    dv_low[...] = dv_acc[pl.ds(far, n * rows), :].astype(jnp.bfloat16)

    def spread(s, carry):
        to = lax.rem(me + s, n)
        give(dk_low, gk, 1, to)
        give(dv_low, gv, 2, to)
        return carry

    lax.fori_loop(1, n, spread, 0)
    keep(dk_low, gk, 1).start()
    keep(dv_low, gv, 2).start()

    for a, (src, dst) in enumerate(((dq_low, gq), (dk_low, gk), (dv_low, gv))):
        keep(src, dst, a).wait()
        wait_bytes(out_recv.at[a])

    for a in range(4):
        wait_bytes(in_send.at[a])
    for a in range(3):
        wait_bytes(out_send.at[a])

    @pl.when(blk < groups - 1)
    def _():
        forward(ext_k, 0).wait_send()
        forward(ext_v, 1).wait_send()

    @pl.when(blk > 0)
    def _():
        handing(give_k, back_k, 0).wait_send()
        handing(give_v, back_v, 1).wait_send()


def body(n, groups, queries, keys, values, grad_out, doc_start):
    rows, total = queries.shape
    width = total // n
    far = (MAXB - 1) * rows
    low, wide = jnp.bfloat16, jnp.float32
    here = (n * rows, width)
    reach = (far + n * rows, width)
    out = jax.ShapeDtypeStruct((rows, total), low)
    any_space = pl.BlockSpec(memory_space=pl.ANY)
    vmem = pl.BlockSpec(memory_space=pltpu.VMEM)
    dma = pltpu.SemaphoreType.DMA
    return pl.pallas_call(
        functools.partial(kernel, n, groups, rows, width),
        out_shape=(out, out, out),
        in_specs=[pl.BlockSpec(memory_space=pltpu.SMEM)] + [any_space] * 4,
        out_specs=(vmem, vmem, vmem),
        scratch_shapes=[
            pltpu.VMEM(reach, low), pltpu.VMEM(reach, low),
            pltpu.VMEM(here, low), pltpu.VMEM(here, low),
            pltpu.VMEM(reach, wide), pltpu.VMEM(reach, wide),
            pltpu.VMEM(here, low), pltpu.VMEM(here, low), pltpu.VMEM(here, low),
            pltpu.VMEM((far, width), low), pltpu.VMEM((far, width), low),
            pltpu.VMEM((far, width), low), pltpu.VMEM((far, width), low),
            dma((4,)), dma((4,)), dma((4,)), dma((2,)), dma((2,)), dma((2,)), dma((2,)),
            dma((3,)), dma((3,)), dma((3,)),
        ],
        compiler_params=pltpu.CompilerParams(
            collective_id=0, has_side_effects=True, vmem_limit_bytes=48 * 1024 * 1024
        ),
    )(doc_start, queries, keys, values, grad_out)


def solution(mesh):
    split = P(("blk", "uly"), None)
    return jax.shard_map(
        functools.partial(body, mesh.shape["uly"], mesh.shape["blk"]),
        mesh=mesh,
        in_specs=(split, split, split, split, P()),
        out_specs=(split, split, split),
        check_vma=False,
    )
```

```python
import functools
import math

import jax
import jax.numpy as jnp
from jax import lax
from jax.experimental import pallas as pl
from jax.experimental.pallas import tpu as pltpu
from jax.sharding import PartitionSpec as P

MAXB = 8
MESH = pl.DeviceIdType.MESH


def nt_dot(a, b):
    return lax.dot_general(a, b, (((1,), (1,)), ((), ())), preferred_element_type=jnp.float32)


def tn_dot(a, b):
    return lax.dot_general(a, b, (((0,), (0,)), ((), ())), preferred_element_type=jnp.float32)


def nn_dot(a, b):
    return lax.dot_general(a, b, (((1,), (0,)), ((), ())), preferred_element_type=jnp.float32)


def kernel(
    n, groups, rows, width,
    docs_in, q_in, k_in, v_in, d_in,
    gq, gk, gv,
    docs, prob_all, ext_k, ext_v, q_all, d_all, dk_acc, dv_acc, dq_low, dk_low, dv_low,
    give_k, give_v, back_k, back_v,
    docs_sem, own_sem, in_send, in_recv, far_send, far_recv, back_send, back_recv,
    out_own, out_send, out_recv,
):
    blk = lax.axis_index("blk")
    me = lax.axis_index("uly")
    reach = MAXB - 1
    far = reach * rows
    tail = far + (n - reach) * rows
    scale = 1.0 / math.sqrt(width)

    barrier = pltpu.get_barrier_semaphore()
    fetch_docs = pltpu.make_async_copy(docs_in, docs, docs_sem)
    fetch_docs.start()

    def greet(s, carry):
        pl.semaphore_signal(
            barrier, inc=1, device_id=(blk, lax.rem(me + s, n)), device_id_type=MESH
        )
        return carry

    lax.fori_loop(1, n, greet, 0)

    beside = sorted({1, groups - 1} - {0, groups})
    for by in beside:
        pl.semaphore_signal(
            barrier, inc=1, device_id=(lax.rem(blk + by, groups), me), device_id_type=MESH
        )

    def columns(ref, head):
        return ref.at[:, pl.ds(pl.multiple_of(head * width, width), width)]

    def block(ref, base, index):
        return ref.at[pl.ds(pl.multiple_of(base + index * rows, rows), rows), :]

    streams = ((k_in, ext_k, far), (q_in, q_all, 0), (v_in, ext_v, far), (d_in, d_all, 0))

    own = [
        pltpu.make_async_copy(columns(src, me), block(dst, base, me), own_sem.at[a])
        for a, (src, dst, base) in enumerate(streams)
    ]
    for copy in own:
        copy.start()

    pl.semaphore_wait(barrier, n - 1 + len(beside))

    for a, (src, dst, base) in enumerate(streams):
        def send(s, carry, a=a, src=src, dst=dst, base=base):
            to = lax.rem(me + s, n)
            pltpu.make_async_remote_copy(
                src_ref=columns(src, to),
                dst_ref=block(dst, base, me),
                send_sem=in_send.at[a],
                recv_sem=in_recv.at[a],
                device_id=(blk, to),
                device_id_type=MESH,
            ).start()
            return carry

        lax.fori_loop(1, n, send, 0)

    dk_acc[...] = jnp.zeros_like(dk_acc)
    dv_acc[...] = jnp.zeros_like(dv_acc)

    @pl.when(blk == 0)
    def _():
        ext_k[pl.ds(0, far), :] = jnp.zeros((far, width), ext_k.dtype)
        ext_v[pl.ds(0, far), :] = jnp.zeros((far, width), ext_v.dtype)

    def wait_bytes(sem):
        part = q_all.at[pl.ds(0, (n - 1) * rows), :]
        pltpu.make_async_copy(part, part, sem).wait()

    def forward(ref, a):
        return pltpu.make_async_remote_copy(
            src_ref=ref.at[pl.ds(tail, far), :],
            dst_ref=ref.at[pl.ds(0, far), :],
            send_sem=far_send.at[a],
            recv_sem=far_recv.at[a],
            device_id=(blk + 1, me),
            device_id_type=MESH,
        )

    def arrived(a):
        own[a].wait()
        wait_bytes(in_recv.at[a])

    arrived(0)

    @pl.when(blk < groups - 1)
    def _():
        forward(ext_k, 0).start()

    arrived(1)
    fetch_docs.wait()

    @pl.when(blk > 0)
    def _():
        forward(ext_k, 0).wait_recv()

    window = MAXB * rows
    key_at = lax.broadcasted_iota(jnp.int32, (rows, rows), 0)
    query_at = lax.broadcasted_iota(jnp.int32, (rows, rows), 1)

    def soften(i, carry):
        q = q_all[pl.ds(pl.multiple_of(i * rows, rows), rows), :]
        k = ext_k[pl.ds(pl.multiple_of(i * rows, rows), window), :]
        score = nt_dot(k, q)
        mine = blk * n + i
        doc = docs[mine]
        parts = []
        for t in range(reach):
            other = mine - reach + t
            same = (docs[jnp.maximum(other, 0)] == doc) & (other >= 0)
            parts.append(score[t * rows : (t + 1) * rows] + jnp.where(same, 0.0, -1e30))
        parts.append(jnp.where(key_at <= query_at, score[reach * rows :], -1e30))
        score = jnp.concatenate(parts, 0)
        top = jnp.max(score, axis=0, keepdims=True)
        weight = jnp.exp((score - top) * scale)
        share = 1.0 / jnp.sum(weight, axis=0, keepdims=True)
        prob_all[pl.ds(pl.multiple_of(i * window, window), window), :] = weight * share
        return carry

    lax.fori_loop(0, n, soften, 0)

    arrived(2)

    @pl.when(blk < groups - 1)
    def _():
        forward(ext_v, 1).start()

    arrived(3)

    @pl.when(blk > 0)
    def _():
        forward(ext_v, 1).wait_recv()

    def attend(i):
        here = pl.ds(pl.multiple_of(i * rows, rows), rows)
        span = pl.ds(pl.multiple_of(i * rows, rows), window)
        q = q_all[here, :]
        d = d_all[here, :]
        k = ext_k[span, :]
        dprob = nt_dot(ext_v[span, :], d)
        prob = prob_all[pl.ds(pl.multiple_of(i * window, window), window), :]
        delta = jnp.sum(prob * dprob, axis=0, keepdims=True)
        dscore = (prob * ((dprob - delta) * scale)).astype(jnp.bfloat16)
        dv_acc[span, :] += nn_dot(prob.astype(jnp.bfloat16), d)
        dk_acc[span, :] += nn_dot(dscore, q)
        dq_low[here, :] = tn_dot(dscore, k).astype(jnp.bfloat16)

    def give(src, dst, a, i):
        @pl.when(i != me)
        def _():
            pltpu.make_async_remote_copy(
                src_ref=block(src, 0, i),
                dst_ref=columns(dst, me),
                send_sem=out_send.at[a],
                recv_sem=out_recv.at[a],
                device_id=(blk, i),
                device_id_type=MESH,
            ).start()

    def keep(src, dst, a):
        return pltpu.make_async_copy(block(src, 0, me), columns(dst, me), out_own.at[a])

    def run(first, count):
        def order(s):
            return first + lax.rem(me + s, count)

        def step(s, carry):
            @pl.when(s > 0)
            def _():
                give(dq_low, gq, 0, order(s + count - 1))

            attend(order(s))
            return carry

        lax.fori_loop(0, count, step, 0)
        give(dq_low, gq, 0, order(count - 1))

    run(0, reach)

    def handing(src, dst, a):
        return pltpu.make_async_remote_copy(
            src_ref=src,
            dst_ref=dst,
            send_sem=back_send.at[a],
            recv_sem=back_recv.at[a],
            device_id=(blk - 1, me),
            device_id_type=MESH,
        )

    @pl.when(blk > 0)
    def _():
        give_k[...] = dk_acc[pl.ds(0, far), :].astype(jnp.bfloat16)
        give_v[...] = dv_acc[pl.ds(0, far), :].astype(jnp.bfloat16)
        handing(give_k, back_k, 0).start()
        handing(give_v, back_v, 1).start()

    run(reach, n - reach)

    keep(dq_low, gq, 0).start()

    @pl.when(blk < groups - 1)
    def _():
        handing(give_k, back_k, 0).wait_recv()
        handing(give_v, back_v, 1).wait_recv()

    def settle(j):
        here = pl.ds(pl.multiple_of(j * rows, rows), rows)
        there = pl.ds(pl.multiple_of(far + j * rows, rows), rows)

        @pl.when((blk < groups - 1) & (j >= n - reach))
        def _():
            late = pl.ds(pl.multiple_of((j - (n - reach)) * rows, rows), rows)
            dk_acc[there, :] += back_k[late, :].astype(jnp.float32)
            dv_acc[there, :] += back_v[late, :].astype(jnp.float32)

        dk_low[here, :] = dk_acc[there, :].astype(jnp.bfloat16)
        dv_low[here, :] = dv_acc[there, :].astype(jnp.bfloat16)

    settle(lax.rem(me + 1, n))

    def spread(s, carry):
        to = lax.rem(me + s, n)
        settle(lax.rem(me + s + 1, n))
        give(dk_low, gk, 1, to)
        give(dv_low, gv, 2, to)
        return carry

    lax.fori_loop(1, n, spread, 0)
    keep(dk_low, gk, 1).start()
    keep(dv_low, gv, 2).start()

    for a, (src, dst) in enumerate(((dq_low, gq), (dk_low, gk), (dv_low, gv))):
        keep(src, dst, a).wait()
        wait_bytes(out_recv.at[a])

    for a in range(4):
        wait_bytes(in_send.at[a])
    for a in range(3):
        wait_bytes(out_send.at[a])

    @pl.when(blk < groups - 1)
    def _():
        forward(ext_k, 0).wait_send()
        forward(ext_v, 1).wait_send()

    @pl.when(blk > 0)
    def _():
        handing(give_k, back_k, 0).wait_send()
        handing(give_v, back_v, 1).wait_send()


def deliver(a_in, b_in, c_in, a_out, b_out, c_out, sems):
    copies = [
        pltpu.make_async_copy(src, dst, sems.at[i])
        for i, (src, dst) in enumerate(((a_in, a_out), (b_in, b_out), (c_in, c_out)))
    ]
    for copy in copies:
        copy.start()
    for copy in copies:
        copy.wait()


def body(n, groups, queries, keys, values, grad_out, doc_start):
    rows, total = queries.shape
    width = total // n
    far = (MAXB - 1) * rows
    low, wide = jnp.bfloat16, jnp.float32
    here = (n * rows, width)
    reach = (far + n * rows, width)
    out = jax.ShapeDtypeStruct((rows, total), low)
    hbm = pl.BlockSpec(memory_space=pltpu.HBM)
    vmem = pl.BlockSpec(memory_space=pltpu.VMEM)
    dma = pltpu.SemaphoreType.DMA
    grads = pl.pallas_call(
        functools.partial(kernel, n, groups, rows, width),
        out_shape=(out, out, out),
        in_specs=[hbm] * 5,
        out_specs=(vmem, vmem, vmem),
        scratch_shapes=[
            pltpu.SMEM(doc_start.shape, jnp.int32),
            pltpu.VMEM((n * MAXB * rows, rows), wide),
            pltpu.VMEM(reach, low), pltpu.VMEM(reach, low),
            pltpu.VMEM(here, low), pltpu.VMEM(here, low),
            pltpu.VMEM(reach, wide), pltpu.VMEM(reach, wide),
            pltpu.VMEM(here, low), pltpu.VMEM(here, low), pltpu.VMEM(here, low),
            pltpu.VMEM((far, width), low), pltpu.VMEM((far, width), low),
            pltpu.VMEM((far, width), low), pltpu.VMEM((far, width), low),
            dma(()), dma((4,)), dma((4,)), dma((4,)),
            dma((2,)), dma((2,)), dma((2,)), dma((2,)),
            dma((3,)), dma((3,)), dma((3,)),
        ],
        compiler_params=pltpu.CompilerParams(
            collective_id=0, has_side_effects=True, vmem_limit_bytes=36 * 1024 * 1024
        ),
    )(doc_start, queries, keys, values, grad_out)
    return pl.pallas_call(
        deliver,
        out_shape=(out, out, out),
        in_specs=[vmem] * 3,
        out_specs=(hbm, hbm, hbm),
        scratch_shapes=[dma((3,))],
    )(*grads)


def solution(mesh):
    split = P(("blk", "uly"), None)
    return jax.shard_map(
        functools.partial(body, mesh.shape["uly"], mesh.shape["blk"]),
        mesh=mesh,
        in_specs=(split, split, split, split, P()),
        out_specs=(split, split, split),
        check_vma=False,
    )
```

```python
import functools
import math

import jax
import jax.numpy as jnp
from jax import lax
from jax.experimental import pallas as pl
from jax.experimental.pallas import tpu as pltpu
from jax.sharding import PartitionSpec as P

MAXB = 8
MESH = pl.DeviceIdType.MESH


def nt_dot(a, b):
    return lax.dot_general(a, b, (((1,), (1,)), ((), ())), preferred_element_type=jnp.float32)


def tn_dot(a, b):
    return lax.dot_general(a, b, (((0,), (0,)), ((), ())), preferred_element_type=jnp.float32)


def nn_dot(a, b):
    return lax.dot_general(a, b, (((1,), (0,)), ((), ())), preferred_element_type=jnp.float32)


def kernel(
    n, groups, rows, width,
    docs_in, q_in, k_in, v_in, d_in,
    gq, gk, gv,
    docs, prob_all, ext_k, ext_v, q_all, d_all, dk_acc, dv_acc, dq_low, dk_low, dv_low,
    give_k, give_v, back_k, back_v,
    docs_sem, own_sem, in_send, in_recv, far_send, far_recv, back_send, back_recv,
    out_own, out_send, out_recv,
):
    blk = lax.axis_index("blk")
    me = lax.axis_index("uly")
    reach = MAXB - 1
    far = reach * rows
    tail = far + (n - reach) * rows
    scale = 1.0 / math.sqrt(width)

    barrier = pltpu.get_barrier_semaphore()
    fetch_docs = pltpu.make_async_copy(docs_in, docs, docs_sem)
    fetch_docs.start()

    def greet(s, carry):
        pl.semaphore_signal(
            barrier, inc=1, device_id=(blk, lax.rem(me + s, n)), device_id_type=MESH
        )
        return carry

    lax.fori_loop(1, n, greet, 0)

    beside = sorted({1, groups - 1} - {0, groups})
    for by in beside:
        pl.semaphore_signal(
            barrier, inc=1, device_id=(lax.rem(blk + by, groups), me), device_id_type=MESH
        )

    def columns(ref, head):
        return ref.at[:, pl.ds(pl.multiple_of(head * width, width), width)]

    def block(ref, base, index):
        return ref.at[pl.ds(pl.multiple_of(base + index * rows, rows), rows), :]

    streams = ((k_in, ext_k, far), (q_in, q_all, 0), (v_in, ext_v, far), (d_in, d_all, 0))

    own = [
        pltpu.make_async_copy(columns(src, me), block(dst, base, me), own_sem.at[a])
        for a, (src, dst, base) in enumerate(streams)
    ]
    for copy in own:
        copy.start()

    pl.semaphore_wait(barrier, n - 1 + len(beside))

    for a, (src, dst, base) in enumerate(streams):
        def send(s, carry, a=a, src=src, dst=dst, base=base):
            to = lax.rem(me + s, n)
            pltpu.make_async_remote_copy(
                src_ref=columns(src, to),
                dst_ref=block(dst, base, me),
                send_sem=in_send.at[a],
                recv_sem=in_recv.at[a],
                device_id=(blk, to),
                device_id_type=MESH,
            ).start()
            return carry

        lax.fori_loop(1, n, send, 0)

    dk_acc[...] = jnp.zeros_like(dk_acc)
    dv_acc[...] = jnp.zeros_like(dv_acc)

    @pl.when(blk == 0)
    def _():
        ext_k[pl.ds(0, far), :] = jnp.zeros((far, width), ext_k.dtype)
        ext_v[pl.ds(0, far), :] = jnp.zeros((far, width), ext_v.dtype)

    def wait_bytes(sem):
        part = q_all.at[pl.ds(0, (n - 1) * rows), :]
        pltpu.make_async_copy(part, part, sem).wait()

    def forward(ref, a):
        return pltpu.make_async_remote_copy(
            src_ref=ref.at[pl.ds(tail, far), :],
            dst_ref=ref.at[pl.ds(0, far), :],
            send_sem=far_send.at[a],
            recv_sem=far_recv.at[a],
            device_id=(blk + 1, me),
            device_id_type=MESH,
        )

    def arrived(a):
        own[a].wait()
        wait_bytes(in_recv.at[a])

    arrived(0)

    @pl.when(blk < groups - 1)
    def _():
        forward(ext_k, 0).start()

    arrived(1)
    fetch_docs.wait()

    @pl.when(blk > 0)
    def _():
        forward(ext_k, 0).wait_recv()

    window = MAXB * rows
    key_at = lax.broadcasted_iota(jnp.int32, (rows, rows), 0)
    query_at = lax.broadcasted_iota(jnp.int32, (rows, rows), 1)

    def soften(i, carry):
        q = q_all[pl.ds(pl.multiple_of(i * rows, rows), rows), :]
        k = ext_k[pl.ds(pl.multiple_of(i * rows, rows), window), :]
        score = nt_dot(k, q)
        mine = blk * n + i
        doc = docs[mine]
        parts = []
        for t in range(reach):
            other = mine - reach + t
            same = (docs[jnp.maximum(other, 0)] == doc) & (other >= 0)
            parts.append(score[t * rows : (t + 1) * rows] + jnp.where(same, 0.0, -1e30))
        parts.append(jnp.where(key_at <= query_at, score[reach * rows :], -1e30))
        score = jnp.concatenate(parts, 0)
        top = jnp.max(score, axis=0, keepdims=True)
        weight = jnp.exp((score - top) * scale)
        share = 1.0 / jnp.sum(weight, axis=0, keepdims=True)
        prob_all[pl.ds(pl.multiple_of(i * window, window), window), :] = weight * share
        return carry

    lax.fori_loop(0, n, soften, 0)

    arrived(2)

    @pl.when(blk < groups - 1)
    def _():
        forward(ext_v, 1).start()

    arrived(3)

    @pl.when(blk > 0)
    def _():
        forward(ext_v, 1).wait_recv()

    def attend(i):
        here = pl.ds(pl.multiple_of(i * rows, rows), rows)
        span = pl.ds(pl.multiple_of(i * rows, rows), window)
        q = q_all[here, :]
        d = d_all[here, :]
        k = ext_k[span, :]
        dprob = nt_dot(ext_v[span, :], d)
        prob = prob_all[pl.ds(pl.multiple_of(i * window, window), window), :]
        delta = jnp.sum(prob * dprob, axis=0, keepdims=True)
        dscore = (prob * ((dprob - delta) * scale)).astype(jnp.bfloat16)
        dv_acc[span, :] += nn_dot(prob.astype(jnp.bfloat16), d)
        dk_acc[span, :] += nn_dot(dscore, q)
        dq_low[here, :] = tn_dot(dscore, k).astype(jnp.bfloat16)

    def give(src, dst, a, i):
        @pl.when(i != me)
        def _():
            pltpu.make_async_remote_copy(
                src_ref=block(src, 0, i),
                dst_ref=columns(dst, me),
                send_sem=out_send.at[a],
                recv_sem=out_recv.at[a],
                device_id=(blk, i),
                device_id_type=MESH,
            ).start()

    def keep(src, dst, a):
        return pltpu.make_async_copy(block(src, 0, me), columns(dst, me), out_own.at[a])

    def run(first, count):
        def order(s):
            return first + lax.rem(me + s, count)

        def step(s, carry):
            @pl.when(s > 0)
            def _():
                give(dq_low, gq, 0, order(s + count - 1))

            attend(order(s))
            return carry

        lax.fori_loop(0, count, step, 0)
        give(dq_low, gq, 0, order(count - 1))

    run(0, reach)

    def handing(src, dst, a):
        return pltpu.make_async_remote_copy(
            src_ref=src,
            dst_ref=dst,
            send_sem=back_send.at[a],
            recv_sem=back_recv.at[a],
            device_id=(blk - 1, me),
            device_id_type=MESH,
        )

    @pl.when(blk > 0)
    def _():
        give_k[...] = dk_acc[pl.ds(0, far), :].astype(jnp.bfloat16)
        give_v[...] = dv_acc[pl.ds(0, far), :].astype(jnp.bfloat16)
        handing(give_k, back_k, 0).start()
        handing(give_v, back_v, 1).start()

    run(reach, n - reach)

    keep(dq_low, gq, 0).start()

    @pl.when(blk < groups - 1)
    def _():
        handing(give_k, back_k, 0).wait_recv()
        handing(give_v, back_v, 1).wait_recv()

    def settle(j):
        here = pl.ds(pl.multiple_of(j * rows, rows), rows)
        there = pl.ds(pl.multiple_of(far + j * rows, rows), rows)

        @pl.when((blk < groups - 1) & (j >= n - reach))
        def _():
            late = pl.ds(pl.multiple_of((j - (n - reach)) * rows, rows), rows)
            dk_acc[there, :] += back_k[late, :].astype(jnp.float32)
            dv_acc[there, :] += back_v[late, :].astype(jnp.float32)

        dk_low[here, :] = dk_acc[there, :].astype(jnp.bfloat16)
        dv_low[here, :] = dv_acc[there, :].astype(jnp.bfloat16)

    settle(lax.rem(me + 1, n))

    def spread(s, carry):
        to = lax.rem(me + s, n)
        settle(lax.rem(me + s + 1, n))
        give(dk_low, gk, 1, to)
        give(dv_low, gv, 2, to)
        return carry

    lax.fori_loop(1, n, spread, 0)
    keep(dk_low, gk, 1).start()
    keep(dv_low, gv, 2).start()

    for a, (src, dst) in enumerate(((dq_low, gq), (dk_low, gk), (dv_low, gv))):
        keep(src, dst, a).wait()
        wait_bytes(out_recv.at[a])

    for a in range(4):
        wait_bytes(in_send.at[a])
    for a in range(3):
        wait_bytes(out_send.at[a])

    @pl.when(blk < groups - 1)
    def _():
        forward(ext_k, 0).wait_send()
        forward(ext_v, 1).wait_send()

    @pl.when(blk > 0)
    def _():
        handing(give_k, back_k, 0).wait_send()
        handing(give_v, back_v, 1).wait_send()


def deliver(a_in, b_in, c_in, a_out, b_out, c_out, sems):
    copies = [
        pltpu.make_async_copy(src, dst, sems.at[i])
        for i, (src, dst) in enumerate(((a_in, a_out), (b_in, b_out), (c_in, c_out)))
    ]
    for copy in copies:
        copy.start()
    for copy in copies:
        copy.wait()


def body(n, groups, queries, keys, values, grad_out, doc_start):
    rows, total = queries.shape
    width = total // n
    far = (MAXB - 1) * rows
    low, wide = jnp.bfloat16, jnp.float32
    here = (n * rows, width)
    reach = (far + n * rows, width)
    out = jax.ShapeDtypeStruct((rows, total), low)
    hbm = pl.BlockSpec(memory_space=pltpu.HBM)
    vmem = pl.BlockSpec(memory_space=pltpu.VMEM)
    dma = pltpu.SemaphoreType.DMA
    grads = pl.pallas_call(
        functools.partial(kernel, n, groups, rows, width),
        out_shape=(out, out, out),
        in_specs=[hbm] * 5,
        out_specs=(hbm, hbm, hbm),
        scratch_shapes=[
            pltpu.SMEM(doc_start.shape, jnp.int32),
            pltpu.VMEM((n * MAXB * rows, rows), wide),
            pltpu.VMEM(reach, low), pltpu.VMEM(reach, low),
            pltpu.VMEM(here, low), pltpu.VMEM(here, low),
            pltpu.VMEM(reach, wide), pltpu.VMEM(reach, wide),
            pltpu.VMEM(here, low), pltpu.VMEM(here, low), pltpu.VMEM(here, low),
            pltpu.VMEM((far, width), low), pltpu.VMEM((far, width), low),
            pltpu.VMEM((far, width), low), pltpu.VMEM((far, width), low),
            dma(()), dma((4,)), dma((4,)), dma((4,)),
            dma((2,)), dma((2,)), dma((2,)), dma((2,)),
            dma((3,)), dma((3,)), dma((3,)),
        ],
        compiler_params=pltpu.CompilerParams(
            collective_id=0, has_side_effects=True, vmem_limit_bytes=56 * 1024 * 1024
        ),
    )(doc_start, queries, keys, values, grad_out)
    return pl.pallas_call(
        deliver,
        out_shape=(out, out, out),
        in_specs=[vmem] * 3,
        out_specs=(hbm, hbm, hbm),
        scratch_shapes=[dma((3,))],
    )(*grads)


def solution(mesh):
    split = P(("blk", "uly"), None)
    return jax.shard_map(
        functools.partial(body, mesh.shape["uly"], mesh.shape["blk"]),
        mesh=mesh,
        in_specs=(split, split, split, split, P()),
        out_specs=(split, split, split),
        check_vma=False,
    )
```

```python
import functools
import math

import jax
import jax.numpy as jnp
from jax import lax
from jax.experimental import pallas as pl
from jax.experimental.pallas import tpu as pltpu
from jax.sharding import PartitionSpec as P

MAXB = 8
MESH = pl.DeviceIdType.MESH


def nt_dot(a, b):
    return lax.dot_general(a, b, (((1,), (1,)), ((), ())), preferred_element_type=jnp.float32)


def tn_dot(a, b):
    return lax.dot_general(a, b, (((0,), (0,)), ((), ())), preferred_element_type=jnp.float32)


def nn_dot(a, b):
    return lax.dot_general(a, b, (((1,), (0,)), ((), ())), preferred_element_type=jnp.float32)


def kernel(
    n, groups, rows, width,
    docs_in, q_in, k_in, v_in, d_in,
    gq, gk, gv,
    docs, prob_all, ext_k, ext_v, q_all, d_all, dk_acc, dv_acc, dq_low, dk_low, dv_low,
    give_k, give_v, back_k, back_v,
    docs_sem, own_sem, in_send, in_recv, far_send, far_recv, back_send, back_recv,
    out_own, out_send, out_recv,
):
    blk = lax.axis_index("blk")
    me = lax.axis_index("uly")
    reach = MAXB - 1
    far = reach * rows
    tail = far + (n - reach) * rows
    scale = 1.0 / math.sqrt(width)

    barrier = pltpu.get_barrier_semaphore()
    fetch_docs = pltpu.make_async_copy(docs_in, docs, docs_sem)
    fetch_docs.start()

    def greet(s, carry):
        pl.semaphore_signal(
            barrier, inc=1, device_id=(blk, lax.rem(me + s, n)), device_id_type=MESH
        )
        return carry

    lax.fori_loop(1, n, greet, 0)

    beside = sorted({1, groups - 1} - {0, groups})
    for by in beside:
        pl.semaphore_signal(
            barrier, inc=1, device_id=(lax.rem(blk + by, groups), me), device_id_type=MESH
        )

    def columns(ref, head):
        return ref.at[:, pl.ds(pl.multiple_of(head * width, width), width)]

    def block(ref, base, index):
        return ref.at[pl.ds(pl.multiple_of(base + index * rows, rows), rows), :]

    streams = ((k_in, ext_k, far), (q_in, q_all, 0), (v_in, ext_v, far), (d_in, d_all, 0))

    own = [
        pltpu.make_async_copy(columns(src, me), block(dst, base, me), own_sem.at[a])
        for a, (src, dst, base) in enumerate(streams)
    ]
    for copy in own:
        copy.start()

    pl.semaphore_wait(barrier, n - 1 + len(beside))

    for a, (src, dst, base) in enumerate(streams):
        def send(s, carry, a=a, src=src, dst=dst, base=base):
            to = lax.rem(me + s, n)
            pltpu.make_async_remote_copy(
                src_ref=columns(src, to),
                dst_ref=block(dst, base, me),
                send_sem=in_send.at[a],
                recv_sem=in_recv.at[a],
                device_id=(blk, to),
                device_id_type=MESH,
            ).start()
            return carry

        lax.fori_loop(1, n, send, 0)

    dk_acc[...] = jnp.zeros_like(dk_acc)
    dv_acc[...] = jnp.zeros_like(dv_acc)

    @pl.when(blk == 0)
    def _():
        ext_k[pl.ds(0, far), :] = jnp.zeros((far, width), ext_k.dtype)
        ext_v[pl.ds(0, far), :] = jnp.zeros((far, width), ext_v.dtype)

    def wait_bytes(sem):
        part = q_all.at[pl.ds(0, (n - 1) * rows), :]
        pltpu.make_async_copy(part, part, sem).wait()

    def forward(ref, a):
        return pltpu.make_async_remote_copy(
            src_ref=ref.at[pl.ds(tail, far), :],
            dst_ref=ref.at[pl.ds(0, far), :],
            send_sem=far_send.at[a],
            recv_sem=far_recv.at[a],
            device_id=(blk + 1, me),
            device_id_type=MESH,
        )

    def arrived(a):
        own[a].wait()
        wait_bytes(in_recv.at[a])

    arrived(0)

    @pl.when(blk < groups - 1)
    def _():
        forward(ext_k, 0).start()

    arrived(1)
    fetch_docs.wait()

    @pl.when(blk > 0)
    def _():
        forward(ext_k, 0).wait_recv()

    window = MAXB * rows
    key_at = lax.broadcasted_iota(jnp.int32, (rows, rows), 0)
    query_at = lax.broadcasted_iota(jnp.int32, (rows, rows), 1)

    def soften(i, carry):
        q = q_all[pl.ds(pl.multiple_of(i * rows, rows), rows), :]
        k = ext_k[pl.ds(pl.multiple_of(i * rows, rows), window), :]
        score = nt_dot(k, q)
        mine = blk * n + i
        doc = docs[mine]
        parts = []
        for t in range(reach):
            other = mine - reach + t
            same = (docs[jnp.maximum(other, 0)] == doc) & (other >= 0)
            parts.append(score[t * rows : (t + 1) * rows] + jnp.where(same, 0.0, -1e30))
        parts.append(jnp.where(key_at <= query_at, score[reach * rows :], -1e30))
        score = jnp.concatenate(parts, 0)
        top = jnp.max(score, axis=0, keepdims=True)
        weight = jnp.exp((score - top) * scale)
        share = 1.0 / jnp.sum(weight, axis=0, keepdims=True)
        prob_all[pl.ds(pl.multiple_of(i * window, window), window), :] = weight * share
        return carry

    lax.fori_loop(0, n, soften, 0)

    arrived(2)

    @pl.when(blk < groups - 1)
    def _():
        forward(ext_v, 1).start()

    arrived(3)

    @pl.when(blk > 0)
    def _():
        forward(ext_v, 1).wait_recv()

    def attend(i):
        here = pl.ds(pl.multiple_of(i * rows, rows), rows)
        span = pl.ds(pl.multiple_of(i * rows, rows), window)
        q = q_all[here, :]
        d = d_all[here, :]
        k = ext_k[span, :]
        dprob = nt_dot(ext_v[span, :], d)
        prob = prob_all[pl.ds(pl.multiple_of(i * window, window), window), :]
        delta = jnp.sum(prob * dprob, axis=0, keepdims=True)
        dscore = (prob * ((dprob - delta) * scale)).astype(jnp.bfloat16)
        dv_acc[span, :] += nn_dot(prob.astype(jnp.bfloat16), d)
        dk_acc[span, :] += nn_dot(dscore, q)
        dq_low[here, :] = tn_dot(dscore, k).astype(jnp.bfloat16)

    def give(src, dst, a, i):
        @pl.when(i != me)
        def _():
            pltpu.make_async_remote_copy(
                src_ref=block(src, 0, i),
                dst_ref=columns(dst, me),
                send_sem=out_send.at[a],
                recv_sem=out_recv.at[a],
                device_id=(blk, i),
                device_id_type=MESH,
            ).start()

    def keep(src, dst, a):
        return pltpu.make_async_copy(block(src, 0, me), columns(dst, me), out_own.at[a])

    def run(first, count):
        def order(s):
            return first + lax.rem(me + s, count)

        def step(s, carry):
            @pl.when(s > 0)
            def _():
                give(dq_low, gq, 0, order(s + count - 1))

            attend(order(s))
            return carry

        lax.fori_loop(0, count, step, 0)
        give(dq_low, gq, 0, order(count - 1))

    run(0, reach)

    def handing(src, dst, a):
        return pltpu.make_async_remote_copy(
            src_ref=src,
            dst_ref=dst,
            send_sem=back_send.at[a],
            recv_sem=back_recv.at[a],
            device_id=(blk - 1, me),
            device_id_type=MESH,
        )

    @pl.when(blk > 0)
    def _():
        give_k[...] = dk_acc[pl.ds(0, far), :].astype(jnp.bfloat16)
        give_v[...] = dv_acc[pl.ds(0, far), :].astype(jnp.bfloat16)
        handing(give_k, back_k, 0).start()
        handing(give_v, back_v, 1).start()

    run(reach, n - reach)

    keep(dq_low, gq, 0).start()

    for a, acc, low, give_far, back, dst in (
        (0, dk_acc, dk_low, give_k, back_k, gk),
        (1, dv_acc, dv_low, give_v, back_v, gv),
    ):
        @pl.when(blk < groups - 1)
        def _(a=a, give_far=give_far, back=back):
            handing(give_far, back, a).wait_recv()

        def settle(j, acc=acc, low=low, back=back):
            here = pl.ds(pl.multiple_of(j * rows, rows), rows)
            there = pl.ds(pl.multiple_of(far + j * rows, rows), rows)

            @pl.when((blk < groups - 1) & (j >= n - reach))
            def _():
                late = pl.ds(pl.multiple_of((j - (n - reach)) * rows, rows), rows)
                acc[there, :] += back[late, :].astype(jnp.float32)

            low[here, :] = acc[there, :].astype(jnp.bfloat16)

        settle(lax.rem(me + 1, n))

        def spread(s, carry, a=a, low=low, dst=dst, settle=settle):
            to = lax.rem(me + s, n)
            settle(lax.rem(me + s + 1, n))
            give(low, dst, a + 1, to)
            return carry

        lax.fori_loop(1, n, spread, 0)
        keep(low, dst, a + 1).start()

    for a, (src, dst) in enumerate(((dq_low, gq), (dk_low, gk), (dv_low, gv))):
        keep(src, dst, a).wait()
        wait_bytes(out_recv.at[a])

    for a in range(4):
        wait_bytes(in_send.at[a])
    for a in range(3):
        wait_bytes(out_send.at[a])

    @pl.when(blk < groups - 1)
    def _():
        forward(ext_k, 0).wait_send()
        forward(ext_v, 1).wait_send()

    @pl.when(blk > 0)
    def _():
        handing(give_k, back_k, 0).wait_send()
        handing(give_v, back_v, 1).wait_send()


def deliver(a_in, b_in, c_in, a_out, b_out, c_out, held, load_sems, store_sems):
    parts = load_sems.shape[0] // 3
    step = held.shape[1] // parts
    loads, stores = [], []
    for i, (src, dst) in enumerate(((a_in, a_out), (b_in, b_out), (c_in, c_out))):
        for c in range(parts):
            at = pl.ds(c * step, step)
            mid, sem = held.at[i, at, :], i * parts + c
            loads.append(pltpu.make_async_copy(src.at[at, :], mid, load_sems.at[sem]))
            stores.append(pltpu.make_async_copy(mid, dst.at[at, :], store_sems.at[sem]))
    for load in loads:
        load.start()
    for load, store in zip(loads, stores):
        load.wait()
        store.start()
    for store in stores:
        store.wait()


def body(n, groups, queries, keys, values, grad_out, doc_start):
    rows, total = queries.shape
    width = total // n
    far = (MAXB - 1) * rows
    low, wide = jnp.bfloat16, jnp.float32
    here = (n * rows, width)
    reach = (far + n * rows, width)
    out = jax.ShapeDtypeStruct((rows, total), low)
    hbm = pl.BlockSpec(memory_space=pltpu.HBM)
    vmem = pl.BlockSpec(memory_space=pltpu.VMEM)
    dma = pltpu.SemaphoreType.DMA
    grads = pl.pallas_call(
        functools.partial(kernel, n, groups, rows, width),
        out_shape=(out, out, out),
        in_specs=[hbm] * 5,
        out_specs=(hbm, hbm, hbm),
        scratch_shapes=[
            pltpu.SMEM(doc_start.shape, jnp.int32),
            pltpu.VMEM((n * MAXB * rows, rows), wide),
            pltpu.VMEM(reach, low), pltpu.VMEM(reach, low),
            pltpu.VMEM(here, low), pltpu.VMEM(here, low),
            pltpu.VMEM(reach, wide), pltpu.VMEM(reach, wide),
            pltpu.VMEM(here, low), pltpu.VMEM(here, low), pltpu.VMEM(here, low),
            pltpu.VMEM((far, width), low), pltpu.VMEM((far, width), low),
            pltpu.VMEM((far, width), low), pltpu.VMEM((far, width), low),
            dma(()), dma((4,)), dma((4,)), dma((4,)),
            dma((2,)), dma((2,)), dma((2,)), dma((2,)),
            dma((3,)), dma((3,)), dma((3,)),
        ],
        compiler_params=pltpu.CompilerParams(
            collective_id=0, has_side_effects=True, vmem_limit_bytes=56 * 1024 * 1024
        ),
    )(doc_start, queries, keys, values, grad_out)
    return pl.pallas_call(
        deliver,
        out_shape=(out, out, out),
        in_specs=[hbm] * 3,
        out_specs=(hbm, hbm, hbm),
        scratch_shapes=[pltpu.VMEM((3, rows, total), low), dma((12,)), dma((12,))],
        compiler_params=pltpu.CompilerParams(vmem_limit_bytes=56 * 1024 * 1024),
    )(*grads)


def solution(mesh):
    split = P(("blk", "uly"), None)
    return jax.shard_map(
        functools.partial(body, mesh.shape["uly"], mesh.shape["blk"]),
        mesh=mesh,
        in_specs=(split, split, split, split, P()),
        out_specs=(split, split, split),
        check_vma=False,
    )
```

```python
import functools
import math

import jax
import jax.numpy as jnp
from jax import lax
from jax.experimental import pallas as pl
from jax.experimental.pallas import tpu as pltpu
from jax.sharding import PartitionSpec as P

MAXB = 8
MESH = pl.DeviceIdType.MESH


def nt_dot(a, b):
    return lax.dot_general(a, b, (((1,), (1,)), ((), ())), preferred_element_type=jnp.float32)


def tn_dot(a, b):
    return lax.dot_general(a, b, (((0,), (0,)), ((), ())), preferred_element_type=jnp.float32)


def nn_dot(a, b):
    return lax.dot_general(a, b, (((1,), (0,)), ((), ())), preferred_element_type=jnp.float32)


def kernel(
    n, groups, rows, width,
    docs_in, q_in, k_in, v_in, d_in,
    gq, gk, gv,
    docs, prob_all, ext_k, ext_v, q_all, d_all, dk_acc, dv_acc, dq_low, dk_low, dv_low,
    give_k, give_v, back_k, back_v,
    docs_sem, d_recv, own_sem, in_send, in_recv, far_send, far_recv, back_send, back_recv,
    out_own, out_send, out_recv,
):
    blk = lax.axis_index("blk")
    me = lax.axis_index("uly")
    reach = MAXB - 1
    far = reach * rows
    tail = far + (n - reach) * rows
    scale = 1.0 / math.sqrt(width)

    barrier = pltpu.get_barrier_semaphore()
    fetch_docs = pltpu.make_async_copy(docs_in, docs, docs_sem)
    fetch_docs.start()

    def greet(s, carry):
        pl.semaphore_signal(
            barrier, inc=1, device_id=(blk, lax.rem(me + s, n)), device_id_type=MESH
        )
        return carry

    lax.fori_loop(1, n, greet, 0)

    beside = sorted({1, groups - 1} - {0, groups})
    for by in beside:
        pl.semaphore_signal(
            barrier, inc=1, device_id=(lax.rem(blk + by, groups), me), device_id_type=MESH
        )

    def columns(ref, head):
        return ref.at[:, pl.ds(pl.multiple_of(head * width, width), width)]

    def block(ref, base, index):
        return ref.at[pl.ds(pl.multiple_of(base + index * rows, rows), rows), :]

    streams = ((k_in, ext_k, far), (q_in, q_all, 0), (v_in, ext_v, far), (d_in, d_all, 0))

    own = [
        pltpu.make_async_copy(columns(src, me), block(dst, base, me), own_sem.at[a])
        for a, (src, dst, base) in enumerate(streams)
    ]
    for copy in own:
        copy.start()

    pl.semaphore_wait(barrier, n - 1 + len(beside))

    for a, (src, dst, base) in enumerate(streams):
        def send(s, carry, a=a, src=src, dst=dst, base=base):
            to = lax.rem(me + s, n)
            pltpu.make_async_remote_copy(
                src_ref=columns(src, to),
                dst_ref=block(dst, base, me),
                send_sem=in_send.at[a],
                recv_sem=d_recv.at[me] if a == 3 else in_recv.at[a],
                device_id=(blk, to),
                device_id_type=MESH,
            ).start()
            return carry

        lax.fori_loop(1, n, send, 0)

    dk_acc[...] = jnp.zeros_like(dk_acc)
    dv_acc[...] = jnp.zeros_like(dv_acc)

    @pl.when(blk == 0)
    def _():
        ext_k[pl.ds(0, far), :] = jnp.zeros((far, width), ext_k.dtype)
        ext_v[pl.ds(0, far), :] = jnp.zeros((far, width), ext_v.dtype)

    def wait_bytes(sem):
        part = q_all.at[pl.ds(0, (n - 1) * rows), :]
        pltpu.make_async_copy(part, part, sem).wait()

    def forward(ref, a):
        return pltpu.make_async_remote_copy(
            src_ref=ref.at[pl.ds(tail, far), :],
            dst_ref=ref.at[pl.ds(0, far), :],
            send_sem=far_send.at[a],
            recv_sem=far_recv.at[a],
            device_id=(blk + 1, me),
            device_id_type=MESH,
        )

    def arrived(a):
        own[a].wait()
        wait_bytes(in_recv.at[a])

    arrived(0)

    @pl.when(blk < groups - 1)
    def _():
        forward(ext_k, 0).start()

    arrived(1)
    fetch_docs.wait()

    @pl.when(blk > 0)
    def _():
        forward(ext_k, 0).wait_recv()

    window = MAXB * rows
    key_at = lax.broadcasted_iota(jnp.int32, (rows, rows), 0)
    query_at = lax.broadcasted_iota(jnp.int32, (rows, rows), 1)

    def soften(i, carry):
        q = q_all[pl.ds(pl.multiple_of(i * rows, rows), rows), :]
        k = ext_k[pl.ds(pl.multiple_of(i * rows, rows), window), :]
        score = nt_dot(k, q)
        mine = blk * n + i
        doc = docs[mine]
        parts = []
        for t in range(reach):
            other = mine - reach + t
            same = (docs[jnp.maximum(other, 0)] == doc) & (other >= 0)
            parts.append(score[t * rows : (t + 1) * rows] + jnp.where(same, 0.0, -1e30))
        parts.append(jnp.where(key_at <= query_at, score[reach * rows :], -1e30))
        score = jnp.concatenate(parts, 0)
        top = jnp.max(score, axis=0, keepdims=True)
        weight = jnp.exp((score - top) * scale)
        share = 1.0 / jnp.sum(weight, axis=0, keepdims=True)
        prob_all[pl.ds(pl.multiple_of(i * window, window), window), :] = weight * share
        return carry

    lax.fori_loop(0, n, soften, 0)

    arrived(2)

    @pl.when(blk < groups - 1)
    def _():
        forward(ext_v, 1).start()

    @pl.when(blk > 0)
    def _():
        forward(ext_v, 1).wait_recv()

    def attend(i):
        @pl.when(i == me)
        def _():
            own[3].wait()

        @pl.when(i != me)
        def _():
            landed = block(d_all, 0, i)
            pltpu.make_async_copy(landed, landed, d_recv.at[i]).wait()

        here = pl.ds(pl.multiple_of(i * rows, rows), rows)
        span = pl.ds(pl.multiple_of(i * rows, rows), window)
        q = q_all[here, :]
        d = d_all[here, :]
        k = ext_k[span, :]
        dprob = nt_dot(ext_v[span, :], d)
        prob = prob_all[pl.ds(pl.multiple_of(i * window, window), window), :]
        delta = jnp.sum(prob * dprob, axis=0, keepdims=True)
        dscore = (prob * ((dprob - delta) * scale)).astype(jnp.bfloat16)
        dv_acc[span, :] += nn_dot(prob.astype(jnp.bfloat16), d)
        dk_acc[span, :] += nn_dot(dscore, q)
        dq_low[here, :] = tn_dot(dscore, k).astype(jnp.bfloat16)

    def give(src, dst, a, i):
        @pl.when(i != me)
        def _():
            pltpu.make_async_remote_copy(
                src_ref=block(src, 0, i),
                dst_ref=columns(dst, me),
                send_sem=out_send.at[a],
                recv_sem=out_recv.at[a],
                device_id=(blk, i),
                device_id_type=MESH,
            ).start()

    def keep(src, dst, a):
        return pltpu.make_async_copy(block(src, 0, me), columns(dst, me), out_own.at[a])

    def run(first, count):
        shift = -(-(first + 1 + count) // count) * count - first - 1

        def order(s):
            return first + lax.rem(me - s + shift, count)

        def step(s, carry):
            @pl.when(s > 0)
            def _():
                give(dq_low, gq, 0, order(s - 1))

            attend(order(s))
            return carry

        lax.fori_loop(0, count, step, 0)
        give(dq_low, gq, 0, order(count - 1))

    run(0, reach)

    def handing(src, dst, a):
        return pltpu.make_async_remote_copy(
            src_ref=src,
            dst_ref=dst,
            send_sem=back_send.at[a],
            recv_sem=back_recv.at[a],
            device_id=(blk - 1, me),
            device_id_type=MESH,
        )

    @pl.when(blk > 0)
    def _():
        give_k[...] = dk_acc[pl.ds(0, far), :].astype(jnp.bfloat16)
        give_v[...] = dv_acc[pl.ds(0, far), :].astype(jnp.bfloat16)
        handing(give_k, back_k, 0).start()
        handing(give_v, back_v, 1).start()

    run(reach, n - reach)

    keep(dq_low, gq, 0).start()

    for a, acc, low, give_far, back, dst in (
        (0, dk_acc, dk_low, give_k, back_k, gk),
        (1, dv_acc, dv_low, give_v, back_v, gv),
    ):
        @pl.when(blk < groups - 1)
        def _(a=a, give_far=give_far, back=back):
            handing(give_far, back, a).wait_recv()

        def settle(j, acc=acc, low=low, back=back):
            here = pl.ds(pl.multiple_of(j * rows, rows), rows)
            there = pl.ds(pl.multiple_of(far + j * rows, rows), rows)

            @pl.when((blk < groups - 1) & (j >= n - reach))
            def _():
                late = pl.ds(pl.multiple_of((j - (n - reach)) * rows, rows), rows)
                acc[there, :] += back[late, :].astype(jnp.float32)

            low[here, :] = acc[there, :].astype(jnp.bfloat16)

        settle(lax.rem(me + 1, n))

        def spread(s, carry, a=a, low=low, dst=dst, settle=settle):
            to = lax.rem(me + s, n)
            settle(lax.rem(me + s + 1, n))
            give(low, dst, a + 1, to)
            return carry

        lax.fori_loop(1, n, spread, 0)
        keep(low, dst, a + 1).start()

    for a, (src, dst) in enumerate(((dq_low, gq), (dk_low, gk), (dv_low, gv))):
        keep(src, dst, a).wait()
        wait_bytes(out_recv.at[a])

    for a in range(4):
        wait_bytes(in_send.at[a])
    for a in range(3):
        wait_bytes(out_send.at[a])

    @pl.when(blk < groups - 1)
    def _():
        forward(ext_k, 0).wait_send()
        forward(ext_v, 1).wait_send()

    @pl.when(blk > 0)
    def _():
        handing(give_k, back_k, 0).wait_send()
        handing(give_v, back_v, 1).wait_send()


def deliver(a_in, b_in, c_in, a_out, b_out, c_out, held, load_sems, store_sems):
    parts = load_sems.shape[0] // 3
    step = held.shape[1] // parts
    loads, stores = [], []
    for i, (src, dst) in enumerate(((a_in, a_out), (b_in, b_out), (c_in, c_out))):
        for c in range(parts):
            at = pl.ds(c * step, step)
            mid, sem = held.at[i, at, :], i * parts + c
            loads.append(pltpu.make_async_copy(src.at[at, :], mid, load_sems.at[sem]))
            stores.append(pltpu.make_async_copy(mid, dst.at[at, :], store_sems.at[sem]))
    for load in loads:
        load.start()
    for load, store in zip(loads, stores):
        load.wait()
        store.start()
    for store in stores:
        store.wait()


def body(n, groups, queries, keys, values, grad_out, doc_start):
    rows, total = queries.shape
    width = total // n
    far = (MAXB - 1) * rows
    low, wide = jnp.bfloat16, jnp.float32
    here = (n * rows, width)
    reach = (far + n * rows, width)
    out = jax.ShapeDtypeStruct((rows, total), low)
    hbm = pl.BlockSpec(memory_space=pltpu.HBM)
    vmem = pl.BlockSpec(memory_space=pltpu.VMEM)
    dma = pltpu.SemaphoreType.DMA
    grads = pl.pallas_call(
        functools.partial(kernel, n, groups, rows, width),
        out_shape=(out, out, out),
        in_specs=[hbm] * 5,
        out_specs=(hbm, hbm, hbm),
        scratch_shapes=[
            pltpu.SMEM(doc_start.shape, jnp.int32),
            pltpu.VMEM((n * MAXB * rows, rows), wide),
            pltpu.VMEM(reach, low), pltpu.VMEM(reach, low),
            pltpu.VMEM(here, low), pltpu.VMEM(here, low),
            pltpu.VMEM(reach, wide), pltpu.VMEM(reach, wide),
            pltpu.VMEM(here, low), pltpu.VMEM(here, low), pltpu.VMEM(here, low),
            pltpu.VMEM((far, width), low), pltpu.VMEM((far, width), low),
            pltpu.VMEM((far, width), low), pltpu.VMEM((far, width), low),
            dma(()), dma((n,)), dma((4,)), dma((4,)), dma((3,)),
            dma((2,)), dma((2,)), dma((2,)), dma((2,)),
            dma((3,)), dma((3,)), dma((3,)),
        ],
        compiler_params=pltpu.CompilerParams(
            collective_id=0, has_side_effects=True, vmem_limit_bytes=56 * 1024 * 1024
        ),
    )(doc_start, queries, keys, values, grad_out)
    return pl.pallas_call(
        deliver,
        out_shape=(out, out, out),
        in_specs=[hbm] * 3,
        out_specs=(hbm, hbm, hbm),
        scratch_shapes=[pltpu.VMEM((3, rows, total), low), dma((12,)), dma((12,))],
        compiler_params=pltpu.CompilerParams(vmem_limit_bytes=56 * 1024 * 1024),
    )(*grads)


def solution(mesh):
    split = P(("blk", "uly"), None)
    return jax.shard_map(
        functools.partial(body, mesh.shape["uly"], mesh.shape["blk"]),
        mesh=mesh,
        in_specs=(split, split, split, split, P()),
        out_specs=(split, split, split),
        check_vma=False,
    )
```
